32 devices in a mesh: groups: 2 (over x), pool: 8 (over z, y), shard: 2 (over core).
Axes of the slice: x: 2, y: 2, z: 4, core: 2. Of those that a mesh axis runs over, the one named last changes fastest.
Arguments:
- tokens: bfloat16 [2, 64, 8192], P(None, ('groups', 'pool'), 'shard'), parts along dimension 1, may hold values from -6 to 6
- counts: int32 [2, 16], P(None, ('groups', 'pool')), parts along dimension 1, may hold values from 0 to 4, as said below
- gate_up: bfloat16 [8192, 2, 28672], P('shard', None, 'pool'), may hold values from -0.0625 to 0.0625
- down: bfloat16 [28672, 8192], P('pool', 'shard'), may hold values from -0.03125 to 0.03125
Outputs:
- mixed: bfloat16 [2, 64, 8192], P(None, ('groups', 'pool'), 'shard'), parts along dimension 1
The draws below stay inside these ranges and needn't reach their ends.
There are 2 independent parts, one for each index of `groups`. The reference program is written for one: setup_inputs(seed, part) draws one part's arguments, and reference() takes and returns one part's arrays. A program takes and returns all parts, laid end to end along the dimension named above; an argument that names none is the same for every part. Nothing has to cross between parts.
Inputs may be any that keep to these rules, and one draw needn't show every extreme that they name: `counts`: in each micro-batch some device has 4 live rows and some has none.
All inputs are finite; a program needn't handle non-finite values.
Results may differ from the reference program's by a relative error of at most 0.005.
Values may be sent and summed in bfloat16 or wider, within the bound.
A program may use at most 256 MiB of HBM per device.

```python
import jax
import jax.numpy as jnp

D = 8192
FF = 28672
CAP = 4
MICRO = 2
SLOTS = 32
N_POOL = 8


def draw_counts(key, part):
    device_ids = jnp.arange(N_POOL)
    rows = []
    for micro_batch in range(MICRO):
        key_count = jax.random.fold_in(key, 21 + 2 * micro_batch)
        key_order = jax.random.fold_in(key, 22 + 2 * micro_batch)
        drawn = jax.random.randint(key_count, (N_POOL,), 0, CAP + 1)
        order = jax.random.permutation(key_order, N_POOL)
        drawn = jnp.where(device_ids == order[0], CAP, drawn)
        drawn = jnp.where(device_ids == order[1], 0, drawn)
        rows.append(drawn)
    return jnp.stack(rows).astype(jnp.int32)


def levels(rng, shape, pieces, least, top_value):
    loudness, own = 1.0, jax.random.fold_in(rng, 6)
    for axis_at, blocks in pieces:
        heights = jnp.exp(jax.random.uniform(jax.random.fold_in(own, axis_at), (blocks,), jnp.float32, least / len(pieces), top_value / len(pieces)))
        loudness = loudness * jnp.repeat(heights, shape[axis_at] // blocks).reshape([-1 if axis == axis_at else 1 for axis in range(len(shape))])
    return loudness


def bell_draw(rng, shape, scale, most, shards=(), kind=jnp.bfloat16):
    array = jax.random.normal(rng, shape, jnp.float32) * scale
    if len(shards) > 0:
        array = levels(rng, shape, shards, -0.22, 0.18) * array
    return jnp.clip(array, min=-most, max=most).astype(kind)


def setup_inputs(seed: int = 0, part: int = 0) -> dict:
    arg_keys = jax.random.split(jax.random.key(seed), 5)
    part_keys = jax.random.split(jax.random.fold_in(arg_keys[4], part), 5)
    tokens = bell_draw(part_keys[0], (MICRO, SLOTS, D), 1.0, 6.0, ((1, 8), (2, 2)))
    counts = draw_counts(jax.random.fold_in(jax.random.fold_in(arg_keys[4], part), 71), part)
    gate_up = bell_draw(arg_keys[2], (D, 2, FF), D ** -0.5, 0.0625, ((0, 2), (2, 8)))
    down = bell_draw(arg_keys[3], (FF, D), FF ** -0.5, 0.03125, ((0, 8), (1, 2)))
    return dict(tokens=tokens, counts=counts, gate_up=gate_up, down=down)


def reference(tokens, counts, gate_up, down):
    slot_index = jnp.arange(SLOTS, dtype=jnp.int32)
    owner_index = slot_index // CAP
    position = slot_index % CAP
    flat_weights = gate_up.reshape(D, 2 * FF)
    outputs = []
    for micro_batch in range(MICRO):
        live_mask = position < counts[micro_batch][owner_index]
        live_rows = jnp.where(live_mask[:, None], tokens[micro_batch], jnp.zeros((), tokens.dtype))
        projections = jnp.dot(live_rows, flat_weights, preferred_element_type=jnp.float32).reshape(SLOTS, 2, FF)
        hidden = (jax.nn.silu(projections[:, 0]) * projections[:, 1]).astype(jnp.bfloat16)
        mixed_rows = jnp.dot(hidden, down, preferred_element_type=jnp.float32)
        outputs.append(jnp.where(live_mask[:, None], mixed_rows, 0.0).astype(jnp.bfloat16))
    return jnp.stack(outputs)
```

```python
import functools

import jax
import jax.numpy as jnp
from jax import lax
from jax.experimental import pallas as pl
from jax.experimental.pallas import tpu as pltpu
from jax.sharding import PartitionSpec as P

MESH = pl.DeviceIdType.MESH
F32 = jnp.float32
BF16 = jnp.bfloat16


def layer(
    pool, slow, fast, depth, width, ring, pieces,
    counts_ref, tokens_ref, gate_up_ref, down_ref, out_ref,
    rows_in, rows_wide, sums, sent, got, hidden, gate_buf, down_buf,
    mixed, pair_out, pair_in, slow_out, slow_in,
    own_sem, gate_sem, down_sem,
    rows_send, rows_recv, side_send, side_recv,
    half_send, half_recv, pair_send, pair_recv, slow_send, slow_recv,
):
    micro, capacity, features = tokens_ref.shape
    units = gate_up_ref.shape[2]
    columns = down_ref.shape[1]
    block = micro * capacity
    total = pool * block
    gate_steps = features // depth
    down_steps = columns // width
    me = lax.axis_index("pool")
    core = lax.axis_index("shard")
    at_slow = me // fast
    at_fast = lax.rem(me, fast)
    beside = at_slow * fast + (1 - at_fast)

    def slow_peer(step):
        return lax.rem(at_slow + step, slow)

    def slow_source(step):
        return lax.rem(at_slow + slow - step, slow)

    def gate_copy(step):
        slot = lax.rem(step, ring)
        start = pl.multiple_of(step * depth, depth)
        return pltpu.make_async_copy(
            gate_up_ref.at[pl.ds(start, depth)], gate_buf.at[slot], gate_sem.at[slot]
        )

    def down_copy(step):
        start = pl.multiple_of(step * width, width)
        return pltpu.make_async_copy(
            down_ref.at[:, pl.ds(start, width)], down_buf.at[step], down_sem.at[step]
        )

    own = pltpu.make_async_copy(tokens_ref, rows_in.at[me], own_sem)
    own.start()
    for step in range(ring):
        gate_copy(step).start()

    barrier = pltpu.get_barrier_semaphore()
    for step in range(1, slow):
        pl.semaphore_signal(
            barrier, inc=1, device_id={"pool": slow_peer(step) * fast + at_fast}, device_id_type=MESH
        )
    pl.semaphore_signal(barrier, inc=1, device_id={"pool": beside}, device_id_type=MESH)
    pl.semaphore_signal(barrier, inc=1, device_id={"shard": 1 - core}, device_id_type=MESH)
    pl.semaphore_wait(barrier, slow + 1)

    row_copies = []
    for step in range(1, slow):
        copy = pltpu.make_async_remote_copy(
            src_ref=tokens_ref,
            dst_ref=rows_in.at[me],
            send_sem=rows_send.at[step - 1],
            recv_sem=rows_recv.at[step - 1],
            device_id={"pool": slow_peer(step) * fast + at_fast},
            device_id_type=MESH,
        )
        copy.start()
        row_copies.append(copy)
    first = pltpu.make_async_remote_copy(
        src_ref=tokens_ref,
        dst_ref=rows_in.at[me],
        send_sem=side_send.at[0],
        recv_sem=side_recv.at[0],
        device_id={"pool": beside},
        device_id_type=MESH,
    )
    first.start()
    side_copies = [first]
    sums[...] = jnp.zeros_like(sums)
    for step in range(1, slow):
        row_copies[step - 1].wait_recv()
        source = slow_source(step) * fast + at_fast
        copy = pltpu.make_async_remote_copy(
            src_ref=rows_in.at[source],
            dst_ref=rows_in.at[source],
            send_sem=side_send.at[step],
            recv_sem=side_recv.at[step],
            device_id={"pool": beside},
            device_id_type=MESH,
        )
        copy.start()
        side_copies.append(copy)
    own.wait()
    for copy in side_copies:
        copy.wait()
    for copy in row_copies:
        copy.wait_send()

    lane = lax.broadcasted_iota(jnp.int32, (128, 256), 1)
    place = lax.broadcasted_iota(jnp.int32, (128, 256), 0)
    even = jnp.where(lane == 2 * place, 1.0, 0.0).astype(BF16)
    odd = jnp.where(lane == 2 * place + 1, 1.0, 0.0).astype(BF16)

    def widen(index, carry):
        start = pl.multiple_of(index * 128, 128)
        to = pl.multiple_of(index * 256, 256)
        part = rows_in[:, :, :, pl.ds(start, 128)].reshape(total, 128)
        rows_wide[:total, pl.ds(to, 256)] = jnp.dot(
            part, even, preferred_element_type=F32
        ).astype(BF16)
        rows_wide[total:, pl.ds(to, 256)] = jnp.dot(
            part, odd, preferred_element_type=F32
        ).astype(BF16)
        return carry

    lax.fori_loop(0, features // 128, widen, 0)

    tile = 512

    def project(step, carry):
        gate_copy(step).wait()
        slot = lax.rem(step, ring)
        start = pl.multiple_of(step * 2 * depth, 2 * depth)
        left = rows_wide[:, pl.ds(start, 2 * depth)]
        for at in range(0, units, tile):
            upto = min(at + tile, units)
            weights = gate_buf[slot, :, :, at:upto].reshape(2 * depth, upto - at)
            sums[:, at:upto] += jnp.dot(left, weights, preferred_element_type=F32)

        @pl.when(step + ring < gate_steps)
        def _():
            gate_copy(step + ring).start()

        @pl.when((step + ring >= gate_steps) & (step + ring < gate_steps + down_steps))
        def _():
            down_copy(step + ring - gate_steps).start()

        return carry

    lax.fori_loop(0, gate_steps, project, 0)
    for step in range(ring, down_steps):
        down_copy(step).start()

    span = units // pieces
    halves = []
    for piece in range(pieces):
        at = slice(piece * span, (piece + 1) * span)
        sent[piece] = sums[:, at].astype(BF16)
        copy = pltpu.make_async_remote_copy(
            src_ref=sent.at[piece],
            dst_ref=got.at[piece],
            send_sem=half_send.at[piece],
            recv_sem=half_recv.at[piece],
            device_id={"shard": 1 - core},
            device_id_type=MESH,
        )
        copy.start()
        halves.append(copy)
    for piece in range(pieces):
        at = slice(piece * span, (piece + 1) * span)
        halves[piece].wait()
        gate = sums[:total, at] + got[piece, :total].astype(F32)
        up = sums[total:, at] + got[piece, total:].astype(F32)
        hidden[:, at] = (gate / (1.0 + jnp.exp(-gate)) * up).astype(BF16)

    def pair_copy(step):
        return pltpu.make_async_remote_copy(
            src_ref=pair_out.at[step],
            dst_ref=pair_in.at[step],
            send_sem=pair_send.at[step],
            recv_sem=pair_recv.at[step],
            device_id={"pool": beside},
            device_id_type=MESH,
        )

    def slow_copy(step, ahead):
        return pltpu.make_async_remote_copy(
            src_ref=slow_out.at[step, slow_peer(ahead)],
            dst_ref=slow_in.at[step, ahead - 1],
            send_sem=slow_send.at[step, ahead - 1],
            recv_sem=slow_recv.at[step, ahead - 1],
            device_id={"pool": slow_peer(ahead) * fast + at_fast},
            device_id_type=MESH,
        )

    def spread(step):
        pair_copy(step).wait()
        joined = mixed[step, :, at_fast] + pair_in[step].astype(F32)
        slow_out[step] = joined.astype(BF16)
        for ahead in range(1, slow):
            slow_copy(step, ahead).start()

    def combine(step, carry):
        down_copy(step).wait()
        product = jnp.dot(hidden[...], down_buf[step], preferred_element_type=F32)
        mixed[step] = product.reshape(slow, fast, block, width)
        pair_out[step] = mixed[step, :, 1 - at_fast].astype(BF16)
        pair_copy(step).start()

        @pl.when(step >= 1)
        def _():
            spread(step - 1)

        return carry

    lax.fori_loop(0, down_steps, combine, 0)
    spread(down_steps - 1)

    position = lax.broadcasted_iota(jnp.int32, (capacity, width), 0)

    def finish(step, carry):
        for ahead in range(1, slow):
            slow_copy(step, ahead).wait()
        value = mixed[step, at_slow, at_fast] + pair_in[step, at_slow].astype(F32)
        for ahead in range(1, slow):
            value = value + slow_in[step, ahead - 1].astype(F32)
        start = pl.multiple_of(step * width, width)
        for index in range(micro):
            part = value[index * capacity : (index + 1) * capacity]
            live = position < counts_ref[index, 0]
            out_ref[index, :, pl.ds(start, width)] = jnp.where(live, part, 0.0).astype(BF16)
        return carry

    lax.fori_loop(0, down_steps, finish, 0)


def solution(mesh):
    pool = mesh.shape["pool"]
    fast = 2
    slow = pool // fast
    placed = (
        P(None, ("groups", "pool"), "shard"),
        P(None, ("groups", "pool")),
        P("shard", None, "pool"),
        P("pool", "shard"),
    )

    def shards(tokens, counts, gate_up, down):
        micro, capacity, features = tokens.shape
        units = gate_up.shape[2]
        columns = down.shape[1]
        depth = 256
        width = 512
        ring = 7
        pieces = 4 if units % 512 == 0 else 1
        block = micro * capacity
        total = pool * block
        steps = columns // width
        dma = pltpu.SemaphoreType.DMA
        return pl.pallas_call(
            functools.partial(layer, pool, slow, fast, depth, width, ring, pieces),
            out_shape=jax.ShapeDtypeStruct(tokens.shape, tokens.dtype),
            in_specs=[
                pl.BlockSpec(memory_space=pltpu.SMEM),
                pl.BlockSpec(memory_space=pl.ANY),
                pl.BlockSpec(memory_space=pl.ANY),
                pl.BlockSpec(memory_space=pl.ANY),
            ],
            out_specs=pl.BlockSpec(memory_space=pltpu.VMEM),
            scratch_shapes=[
                pltpu.VMEM((pool, micro, capacity, features), BF16),
                pltpu.VMEM((2 * total, 2 * features), BF16),
                pltpu.VMEM((2 * total, units), F32),
                pltpu.VMEM((pieces, 2 * total, units // pieces), BF16),
                pltpu.VMEM((pieces, 2 * total, units // pieces), BF16),
                pltpu.VMEM((total, units), BF16),
                pltpu.VMEM((ring, depth, 2, units), BF16),
                pltpu.VMEM((steps, units, width), BF16),
                pltpu.VMEM((steps, slow, fast, block, width), F32),
                pltpu.VMEM((steps, slow, block, width), BF16),
                pltpu.VMEM((steps, slow, block, width), BF16),
                pltpu.VMEM((steps, slow, block, width), BF16),
                pltpu.VMEM((steps, slow - 1, block, width), BF16),
                dma,
                dma((ring,)),
                dma((steps,)),
                dma((slow - 1,)),
                dma((slow - 1,)),
                dma((slow,)),
                dma((slow,)),
                dma((pieces,)),
                dma((pieces,)),
                dma((steps,)),
                dma((steps,)),
                dma((steps, slow - 1)),
                dma((steps, slow - 1)),
            ],
            compiler_params=pltpu.CompilerParams(
                collective_id=0, has_side_effects=True, vmem_limit_bytes=67043328
            ),
        )(counts, tokens, gate_up, down)

    return jax.shard_map(
        shards,
        mesh=mesh,
        in_specs=placed,
        out_specs=P(None, ("groups", "pool"), "shard"),
        check_vma=False,
    )
```

```python
import functools

import jax
import jax.numpy as jnp
from jax import lax
from jax.experimental import pallas as pl
from jax.experimental.pallas import tpu as pltpu
from jax.sharding import PartitionSpec as P

MESH = pl.DeviceIdType.MESH
F32 = jnp.float32
BF16 = jnp.bfloat16


def layer(
    pool, slow, fast, depth, width, ring, pieces, parts,
    counts_ref, tokens_ref, gate_up_ref, down_ref, out_ref,
    rows_in, rows_wide, sums, got, hidden, gate_buf, down_buf,
    mixed, pair_out, pair_in, slow_out, slow_in,
    own_sem, gate_sem, down_sem,
    rows_send, rows_recv, side_send, side_recv,
    half_send, half_recv, pair_send, pair_recv, slow_send, slow_recv,
):
    micro, capacity, features = tokens_ref.shape
    units = gate_up_ref.shape[2]
    columns = down_ref.shape[1]
    block = micro * capacity
    total = pool * block
    gate_steps = features // depth
    down_steps = columns // width
    me = lax.axis_index("pool")
    core = lax.axis_index("shard")
    at_slow = me // fast
    at_fast = lax.rem(me, fast)
    beside = at_slow * fast + (1 - at_fast)

    def slow_peer(step):
        return lax.rem(at_slow + step, slow)

    def slow_source(step):
        return lax.rem(at_slow + slow - step, slow)

    def gate_copy(step):
        slot = lax.rem(step, ring)
        start = pl.multiple_of(step * depth, depth)
        return pltpu.make_async_copy(
            gate_up_ref.at[pl.ds(start, depth)], gate_buf.at[slot], gate_sem.at[slot]
        )

    def down_copy(step):
        start = pl.multiple_of(step * width, width)
        return pltpu.make_async_copy(
            down_ref.at[:, pl.ds(start, width)], down_buf.at[step], down_sem.at[step]
        )

    own = pltpu.make_async_copy(tokens_ref, rows_in.at[me], own_sem)
    own.start()
    for step in range(ring):
        gate_copy(step).start()

    barrier = pltpu.get_barrier_semaphore()
    for step in range(1, slow):
        pl.semaphore_signal(
            barrier, inc=1, device_id={"pool": slow_peer(step) * fast + at_fast}, device_id_type=MESH
        )
    pl.semaphore_signal(barrier, inc=1, device_id={"pool": beside}, device_id_type=MESH)
    pl.semaphore_signal(barrier, inc=1, device_id={"shard": 1 - core}, device_id_type=MESH)
    pl.semaphore_wait(barrier, slow + 1)

    half = features // parts

    def row_copy(part, step):
        at = pl.ds(part * half, half)
        return pltpu.make_async_remote_copy(
            src_ref=tokens_ref.at[:, :, at],
            dst_ref=rows_in.at[me, :, :, at],
            send_sem=rows_send.at[part, step - 1],
            recv_sem=rows_recv.at[part, step - 1],
            device_id={"pool": slow_peer(step) * fast + at_fast},
            device_id_type=MESH,
        )

    def side_copy(part, step):
        at = pl.ds(part * half, half)
        source = slow_source(step) * fast + at_fast
        place = rows_in.at[source, :, :, at]
        return pltpu.make_async_remote_copy(
            src_ref=tokens_ref.at[:, :, at] if step == 0 else place,
            dst_ref=place,
            send_sem=side_send.at[part, step],
            recv_sem=side_recv.at[part, step],
            device_id={"pool": beside},
            device_id_type=MESH,
        )

    for part in range(parts):
        for step in range(1, slow):
            row_copy(part, step).start()
        side_copy(part, 0).start()
    sums[...] = jnp.zeros_like(sums)

    def forward(part):
        for step in range(1, slow):
            row_copy(part, step).wait()
            side_copy(part, step).start()

    def arrive(part):
        for step in range(slow):
            side_copy(part, step).wait()

    lane = lax.broadcasted_iota(jnp.int32, (128, 256), 1)
    place = lax.broadcasted_iota(jnp.int32, (128, 256), 0)
    even = jnp.where(lane == 2 * place, 1.0, 0.0).astype(BF16)
    odd = jnp.where(lane == 2 * place + 1, 1.0, 0.0).astype(BF16)

    def widen(index, carry):
        start = pl.multiple_of(index * 128, 128)
        to = pl.multiple_of(index * 256, 256)
        part = rows_in[:, :, :, pl.ds(start, 128)].reshape(total, 128)
        rows_wide[:total, pl.ds(to, 256)] = jnp.dot(
            part, even, preferred_element_type=F32
        ).astype(BF16)
        rows_wide[total:, pl.ds(to, 256)] = jnp.dot(
            part, odd, preferred_element_type=F32
        ).astype(BF16)
        return carry

    tile = 512

    def project(step, carry):
        gate_copy(step).wait()
        slot = lax.rem(step, ring)
        start = pl.multiple_of(step * 2 * depth, 2 * depth)
        left = rows_wide[:, pl.ds(start, 2 * depth)]
        for at in range(0, units, tile):
            upto = min(at + tile, units)
            weights = gate_buf[slot, :, :, at:upto].reshape(2 * depth, upto - at)
            sums[:, at:upto] += jnp.dot(left, weights, preferred_element_type=F32)

        @pl.when(step + ring < gate_steps)
        def _():
            gate_copy(step + ring).start()

        @pl.when((step + ring >= gate_steps) & (step + ring < gate_steps + down_steps))
        def _():
            down_copy(step + ring - gate_steps).start()

        return carry

    blocks = half // 128
    share = gate_steps // parts
    forward(0)
    own.wait()
    for part in range(parts):
        arrive(part)
        lax.fori_loop(part * blocks, (part + 1) * blocks, widen, 0, unroll=8)
        if part + 1 < parts:
            forward(part + 1)
        lax.fori_loop(part * share, (part + 1) * share, project, 0)
    for step in range(ring, down_steps):
        down_copy(step).start()

    span = units // pieces
    halves = []
    for piece in range(pieces):
        at = pl.ds(piece * span, span)
        copy = pltpu.make_async_remote_copy(
            src_ref=sums.at[:, at],
            dst_ref=got.at[:, at],
            send_sem=half_send.at[piece],
            recv_sem=half_recv.at[piece],
            device_id={"shard": 1 - core},
            device_id_type=MESH,
        )
        copy.start()
        halves.append(copy)
    for piece in range(pieces):
        at = slice(piece * span, (piece + 1) * span)
        halves[piece].wait()
        gate = sums[:total, at] + got[:total, at]
        up = sums[total:, at] + got[total:, at]
        hidden[:, at] = (gate / (1.0 + jnp.exp(-gate)) * up).astype(BF16)

    def pair_copy(step):
        return pltpu.make_async_remote_copy(
            src_ref=pair_out.at[step],
            dst_ref=pair_in.at[step],
            send_sem=pair_send.at[step],
            recv_sem=pair_recv.at[step],
            device_id={"pool": beside},
            device_id_type=MESH,
        )

    def slow_copy(step, ahead):
        return pltpu.make_async_remote_copy(
            src_ref=slow_out.at[step, slow_peer(ahead)],
            dst_ref=slow_in.at[step, ahead - 1],
            send_sem=slow_send.at[step, ahead - 1],
            recv_sem=slow_recv.at[step, ahead - 1],
            device_id={"pool": slow_peer(ahead) * fast + at_fast},
            device_id_type=MESH,
        )

    def spread(step):
        pair_copy(step).wait()
        joined = mixed[step, :, at_fast] + pair_in[step].astype(F32)
        slow_out[step] = joined.astype(BF16)
        for ahead in range(1, slow):
            slow_copy(step, ahead).start()

    lag = min(3, down_steps)

    def combine(step, carry):
        down_copy(step).wait()
        product = jnp.dot(hidden[...], down_buf[step], preferred_element_type=F32)
        mixed[step] = product.reshape(slow, fast, block, width)
        pair_out[step] = mixed[step, :, 1 - at_fast].astype(BF16)
        pair_copy(step).start()

        @pl.when(step >= lag)
        def _():
            spread(step - lag)

        return carry

    lax.fori_loop(0, down_steps, combine, 0)
    for step in range(down_steps - lag, down_steps):
        spread(step)

    position = lax.broadcasted_iota(jnp.int32, (capacity, width), 0)

    def finish(step, carry):
        for ahead in range(1, slow):
            slow_copy(step, ahead).wait()
        value = mixed[step, at_slow, at_fast] + pair_in[step, at_slow].astype(F32)
        for ahead in range(1, slow):
            value = value + slow_in[step, ahead - 1].astype(F32)
        start = pl.multiple_of(step * width, width)
        for index in range(micro):
            part = value[index * capacity : (index + 1) * capacity]
            live = position < counts_ref[index, 0]
            out_ref[index, :, pl.ds(start, width)] = jnp.where(live, part, 0.0).astype(BF16)
        return carry

    lax.fori_loop(0, down_steps, finish, 0)


def solution(mesh):
    pool = mesh.shape["pool"]
    fast = 2
    slow = pool // fast
    placed = (
        P(None, ("groups", "pool"), "shard"),
        P(None, ("groups", "pool")),
        P("shard", None, "pool"),
        P("pool", "shard"),
    )

    def shards(tokens, counts, gate_up, down):
        micro, capacity, features = tokens.shape
        units = gate_up.shape[2]
        columns = down.shape[1]
        depth = 256
        width = 512
        ring = 7
        pieces = 4 if units % 512 == 0 else 1
        parts = 2
        block = micro * capacity
        total = pool * block
        steps = columns // width
        dma = pltpu.SemaphoreType.DMA
        return pl.pallas_call(
            functools.partial(layer, pool, slow, fast, depth, width, ring, pieces, parts),
            out_shape=jax.ShapeDtypeStruct(tokens.shape, tokens.dtype),
            in_specs=[
                pl.BlockSpec(memory_space=pltpu.SMEM),
                pl.BlockSpec(memory_space=pl.ANY),
                pl.BlockSpec(memory_space=pl.ANY),
                pl.BlockSpec(memory_space=pl.ANY),
            ],
            out_specs=pl.BlockSpec(memory_space=pltpu.VMEM),
            scratch_shapes=[
                pltpu.VMEM((pool, micro, capacity, features), BF16),
                pltpu.VMEM((2 * total, 2 * features), BF16),
                pltpu.VMEM((2 * total, units), F32),
                pltpu.VMEM((2 * total, units), F32),
                pltpu.VMEM((total, units), BF16),
                pltpu.VMEM((ring, depth, 2, units), BF16),
                pltpu.VMEM((steps, units, width), BF16),
                pltpu.VMEM((steps, slow, fast, block, width), F32),
                pltpu.VMEM((steps, slow, block, width), BF16),
                pltpu.VMEM((steps, slow, block, width), BF16),
                pltpu.VMEM((steps, slow, block, width), BF16),
                pltpu.VMEM((steps, slow - 1, block, width), BF16),
                dma,
                dma((ring,)),
                dma((steps,)),
                dma((parts, slow - 1)),
                dma((parts, slow - 1)),
                dma((parts, slow)),
                dma((parts, slow)),
                dma((pieces,)),
                dma((pieces,)),
                dma((steps,)),
                dma((steps,)),
                dma((steps, slow - 1)),
                dma((steps, slow - 1)),
            ],
            compiler_params=pltpu.CompilerParams(
                collective_id=0, has_side_effects=True, vmem_limit_bytes=67043328
            ),
        )(counts, tokens, gate_up, down)

    return jax.shard_map(
        shards,
        mesh=mesh,
        in_specs=placed,
        out_specs=P(None, ("groups", "pool"), "shard"),
        check_vma=False,
    )
```
